32 devices in a mesh: dp: 8 (over y, x, core), space: 4 (over z).
Axes of the slice: x: 2, y: 2, z: 4, core: 2. Of those that a mesh axis runs over, the one named last changes fastest.
Arguments:
- features: bfloat16 [8, 8, 512, 384], P('dp', 'space'), may hold values from -6 to 6
- cotangent: bfloat16 [8, 8, 512, 384], P('dp', 'space'), may hold values from -6 to 6
- weight: bfloat16 [10368, 384], P('dp'), may hold values from -0.0625 to 0.0625
- occupancy: int32 [8, 8, 512], P('dp'), may hold values from 0 to 1, as said below
- neighbours: int32 [8, 8, 27], P('dp'), may hold values from -1 to 7, as said below
- first_moment: float32 [10368, 384], P('dp', 'space'), may hold values from -6 to 6
- second_moment: float32 [10368, 384], P('dp', 'space'), may hold values from 0.01 to 4
Outputs:
- input_grad: bfloat16 [8, 8, 512, 384], P('dp', 'space')
- new_first: float32 [10368, 384], P('dp', 'space')
- new_second: float32 [10368, 384], P('dp', 'space')
The draws below stay inside these ranges and needn't reach their ends.
Inputs may be any that keep to these rules, and one draw needn't show every extreme that they name: `neighbours`: slots s * 2 to s * 2 + 1 of a window lie on index s of space. Exactly 4 slots of each window hold a block, slot 7 always among them, and in every window one index of space has all 2 of its slots holding one. For a slot holding a block, entry 13 is the slot itself and entry 9 e1 + 3 e2 + e3 is the slot of the block displaced by (e1 - 1, e2 - 1, e3 - 1) block widths, or -1 if no block lies there; the relation is symmetric and entries name only slots holding blocks. Every entry of an empty slot is -1. `occupancy`: zero in every slot that holds no block.
All inputs are finite; a program needn't handle non-finite values.
Results may differ from the reference program's by a relative error of at most 0.006.
Values may be sent and summed in bfloat16 or wider, within the bound.
No kernel may reach another device: no remote copies, remote signals or barrier semaphores. Data moves between devices by JAX's collectives and lax.ppermute only.
A program may use at most 192 MiB of HBM per device.

```python
import math
import jax
import jax.numpy as jnp
from jax import lax

C = 384
CAP = 2
WINDOWS = 8
GROUP = 8
N_SPACE = 4


def window_layout(key):
    group_size = N_SPACE * CAP
    live_count = group_size // 2
    key_full, key_order = jax.random.split(key)
    full_device = jax.random.randint(key_full, (), 0, N_SPACE)
    priority = jax.random.permutation(key_order, group_size).astype(jnp.int32)
    slot_ids = jnp.arange(group_size, dtype=jnp.int32)
    scores = priority + group_size * (slot_ids // CAP == full_device).astype(jnp.int32) + 2 * group_size * (slot_ids == group_size - 1).astype(jnp.int32)
    slot_order = jnp.argsort(-scores).astype(jnp.int32)
    cell_ids = jnp.arange(live_count, dtype=jnp.int32)
    cell_x = cell_ids % 2
    cell_y = cell_ids // 2 % 2
    cell_z = cell_ids // 4
    codes = jnp.arange(27, dtype=jnp.int32)
    step_x = codes // 9 - 1
    step_y = codes // 3 % 3 - 1
    step_z = codes % 3 - 1
    near_x = cell_x[:, None] + step_x[None, :]
    near_y = cell_y[:, None] + step_y[None, :]
    near_z = cell_z[:, None] + step_z[None, :]
    inside = (near_x >= 0) & (near_x < 2) & (near_y >= 0) & (near_y < 2) & (near_z >= 0) & (near_z < live_count // 4)
    near_cell = jnp.clip(near_x + 2 * near_y + 4 * near_z, 0, live_count - 1)
    near_slot = jnp.where(inside, jnp.take(slot_order, near_cell), -1).astype(jnp.int32)
    tables = jnp.full((group_size, 27), -1, jnp.int32).at[slot_order[:live_count]].set(near_slot)
    return tables


def window_tables(key):
    return jax.vmap(lambda window_index: window_layout(jax.random.fold_in(key, window_index)))(jnp.arange(WINDOWS))


def draw_neighbours(key, part):
    return window_tables(jax.random.fold_in(key, 11))


def draw_occupancy(key, part):
    tables = window_tables(jax.random.fold_in(key, 11))
    present = tables[:, :, 13] >= 0
    key_dense, key_voxel = jax.random.split(jax.random.fold_in(key, 23))
    thresholds = jax.random.randint(key_dense, (WINDOWS, N_SPACE * CAP), 8, 33)
    voxel_draws = jax.random.randint(key_voxel, (WINDOWS, N_SPACE * CAP, 512), 0, 32)
    filled = (voxel_draws < thresholds[:, :, None]) & present[:, :, None]
    return filled.astype(jnp.int32)


def strengthened(values, own_key, source, target, parts, factor):
    owner, partner = [(jnp.arange(values.shape[axis_at]) // (values.shape[axis_at] // parts)).reshape([-1 if axis == axis_at else 1 for axis in range(values.ndim)]) for axis_at in (source, target)]
    chosen = jax.random.permutation(own_key, parts)[partner]
    strong = (owner == chosen) | (owner == (partner + parts // 2) % parts)
    return jnp.where(strong, factor * values, values)


def shard_levels(own_key, extent, cuts, smallest, high):
    level = 1.0
    for dim, shards_of in cuts:
        steps = jax.random.uniform(jax.random.fold_in(jax.random.fold_in(own_key, 6), dim), (shards_of,), jnp.float32, smallest / len(cuts), high / len(cuts))
        level = level * jnp.repeat(jnp.exp(steps), extent[dim] // shards_of).reshape((-1,) + (1,) * (len(extent) - 1 - dim))
    return level


def scatter_about(stream_key, shape, width, reach, shards=(), kind=jnp.bfloat16):
    factor_of = shard_levels(stream_key, shape, shards, -0.22, 0.18) if shards else 1.0
    result = jax.random.normal(stream_key, shape, jnp.float32) * width * factor_of
    return jnp.minimum(jnp.maximum(result, -reach), reach).astype(kind)


def heavy_noise(key, dims, width, reach, shards, heavy, held_as=jnp.bfloat16):
    values = width * jax.random.normal(key, dims, jnp.float32)
    if shards:
        values = values * shard_levels(key, dims, shards, -0.22, 0.18)
    return jnp.clip(strengthened(values, jax.random.fold_in(key, 3), *heavy), -reach, reach).astype(held_as)


def setup_inputs(seed: int = 0) -> dict:
    key_of = jax.random.split(jax.random.key(seed), 8)
    return {
        "features": heavy_noise(key_of[0], (WINDOWS, GROUP, 512, C), 1.0, 6.0, ((0, 8), (1, 4)), (0, 3, 8, 2.0)),
        "cotangent": heavy_noise(key_of[1], (WINDOWS, GROUP, 512, C), 1.0, 6.0, ((0, 8), (1, 4)), (1, 3, 4, 2.0)),
        "weight": scatter_about(key_of[2], (27 * C, C), (27 * C) ** -0.5, 0.0625, ((0, 8),)),
        "occupancy": draw_occupancy(jax.random.fold_in(key_of[7], 71), 0),
        "neighbours": draw_neighbours(jax.random.fold_in(key_of[7], 71), 0),
        "first_moment": scatter_about(key_of[5], (27 * C, C), 1.0, 6.0, ((0, 8), (1, 4)), jnp.float32),
        "second_moment": jnp.clip(jnp.exp(math.log(4.0) - 5.9914646 * jax.random.uniform(key_of[6], (27 * C, C), jnp.float32) ** shard_levels(key_of[6], (27 * C, C), ((0, 8), (1, 4)), -0.2, 0.2)), 0.01, 4.0),
    }


EDGE_SPANS = ((7, 8), (0, 8), (0, 1))


def build_region(lookup, neighbour_rows):
    slab_list = []
    for first_axis in range(3):
        planes = []
        for second_axis in range(3):
            pieces = []
            for third_axis in range(3):
                offset_code = 9 * first_axis + 3 * second_axis + third_axis
                span_one = EDGE_SPANS[first_axis]
                span_two = EDGE_SPANS[second_axis]
                span_three = EDGE_SPANS[third_axis]
                window_part = lookup[:, span_one[0]:span_one[1], span_two[0]:span_two[1], span_three[0]:span_three[1], :]
                pieces.append(jnp.take(window_part, neighbour_rows[:, offset_code], axis=0))
            planes.append(jnp.concatenate(pieces, axis=3))
        slab_list.append(jnp.concatenate(planes, axis=2))
    return jnp.concatenate(slab_list, axis=1)


def shifted(region, offset):
    first_axis = offset // 9
    second_axis = (offset // 3) % 3
    third_axis = offset % 3
    moved = region[:, first_axis:first_axis + 8, second_axis:second_axis + 8, third_axis:third_axis + 8, :]
    return moved.reshape(-1, region.shape[-1])


def reference(features, cotangent, weight, occupancy, neighbours, first_moment, second_moment):
    channels = features.shape[3]
    group_size = features.shape[1]
    weight_cube = weight.reshape(channels, 27, channels)
    flat_rows = group_size * 512

    def one_window(running, inputs):
        window_feat, window_cot, window_occ, window_links = inputs
        voxel_mask = window_occ.astype(jnp.float32)
        masked = window_feat * window_occ[:, :, None].astype(jnp.bfloat16)
        lookup = jnp.concatenate([masked.reshape(group_size, 8, 8, 8, channels), jnp.zeros((1, 8, 8, 8, channels), jnp.bfloat16)], axis=0)
        slot_links = jnp.where(window_links < 0, group_size, window_links).astype(jnp.int32)
        region = build_region(lookup, slot_links)
        pre = jnp.zeros((flat_rows, channels), jnp.float32)
        for offset in range(27):
            pre = pre + jnp.dot(shifted(region, offset), weight_cube[:, offset, :], preferred_element_type=jnp.float32)
        mask_rows = voxel_mask.reshape(flat_rows, 1)
        cot_rows = window_cot.reshape(flat_rows, channels).astype(jnp.float32)
        sigmoid_pre = jax.nn.sigmoid(pre)
        delta_rows = (cot_rows * mask_rows * sigmoid_pre * (1.0 + pre * (1.0 - sigmoid_pre))).astype(jnp.bfloat16)
        delta_lookup = jnp.concatenate([delta_rows.reshape(group_size, 8, 8, 8, channels), jnp.zeros((1, 8, 8, 8, channels), jnp.bfloat16)], axis=0)
        delta_region = build_region(delta_lookup, slot_links)
        back_rows = jnp.zeros((flat_rows, channels), jnp.float32)
        for offset in range(27):
            back_rows = back_rows + lax.dot_general(shifted(delta_region, 26 - offset), weight_cube[:, offset, :], (((1,), (1,)), ((), ())), preferred_element_type=jnp.float32)
        grad_rows = (cot_rows + mask_rows * back_rows).astype(jnp.bfloat16)
        kernel_terms = [lax.dot_general(shifted(region, offset), delta_rows, (((0,), (0,)), ((), ())), preferred_element_type=jnp.float32) for offset in range(27)]
        kernel_sum = jnp.stack(kernel_terms, axis=1).reshape(27 * channels, channels)
        return running + kernel_sum, grad_rows.reshape(group_size, 512, channels)

    weight_sum, input_grad = lax.scan(one_window, jnp.zeros((27 * channels, channels), jnp.float32), (features, cotangent, occupancy, neighbours))
    scaled_grad = weight_sum / 64.0
    new_first = 0.9 * first_moment + 0.1 * scaled_grad
    new_second = 0.999 * second_moment + 0.001 * scaled_grad * scaled_grad
    return input_grad, new_first, new_second
```

```python
import functools
import itertools

import jax
import jax.numpy as jnp
import numpy as np
from jax import lax
from jax.experimental import pallas as pl
from jax.experimental.pallas import tpu as pltpu
from jax.sharding import PartitionSpec as P


SIDE = 8
PAD = SIDE + 2
VOX = SIDE**3
OFFS = 27
SLAB = SIDE * SIDE
STEPS = 9
LANES = 128
F32 = jnp.float32
BF16 = jnp.bfloat16


def hop_pairs(spatial, capacity):
    group = spatial * capacity
    live = group // 2
    pairs = {}
    for chosen in itertools.combinations(range(group - 1), live - 1):
        slots = chosen + (group - 1,)
        counts = np.bincount([s // capacity for s in slots], minlength=spatial)
        if counts.max() < capacity:
            continue
        for rank, slot in enumerate(slots):
            owner = slot // capacity
            if owner != rank:
                pairs.setdefault(owner - rank, set()).add((owner, rank))
    return {dist: sorted(found) for dist, found in sorted(pairs.items())}


def region_rows():
    c, i, j, l = np.meshgrid(range(3), range(PAD), range(PAD), range(SIDE), indexing="ij")
    coords = (i, j, l + c)
    edges = [np.where(x == 0, 0, np.where(x == PAD - 1, 2, 1)) for x in coords]
    source = [(x - 1) % SIDE for x in coords]
    code = 9 * edges[0] + 3 * edges[1] + edges[2]
    voxel = (source[0] * SIDE + source[1]) * SIDE + source[2]
    place = np.zeros_like(code)
    for x, e in zip(source, edges):
        place = np.where(e == 1, place * SIDE + x, place)
    return tuple(t.reshape(-1).astype(np.int32) for t in (code, voxel, place))


ROW_CODE, ROW_VOXEL, ROW_PLACE = region_rows()
ROWS = ROW_CODE.size
ROWS_C = ROWS // 3


def vmem():
    return pl.BlockSpec(memory_space=pltpu.VMEM)


def params():
    return pltpu.CompilerParams(vmem_limit_bytes=60 * 1024 * 1024)


def cost(flops, nbytes):
    return pl.CostEstimate(flops=int(flops), bytes_accessed=int(nbytes), transcendentals=0)


def shuffle_kernel(w_ref, out_ref, wide):
    rows = out_ref.shape[1]
    for tile in range(wide.shape[0]):
        lanes = slice(tile * LANES, (tile + 1) * LANES)
        wide[tile] = w_ref[:, lanes].astype(F32)
        for k in range(OFFS):
            out_ref[k, :, lanes] = wide[tile, pl.ds(k, rows, stride=OFFS), :].astype(BF16)


def shuffle_weight(weight):
    rows, cout = weight.shape
    return pl.pallas_call(
        shuffle_kernel,
        out_shape=jax.ShapeDtypeStruct((OFFS, rows // OFFS, cout), BF16),
        in_specs=[vmem()],
        out_specs=vmem(),
        scratch_shapes=[pltpu.VMEM((cout // LANES, rows, LANES), F32)],
        compiler_params=params(),
        cost_estimate=cost(0, 4 * rows * cout),
        name="shuffle_weight",
    )(weight)


def place_region(cols_ref, base, pool, store):
    depth = pool.shape[0]
    for c in range(3):
        cols = cols_ref[pl.ds(base + c * ROWS_C, ROWS_C), :]
        picked = (lax.broadcasted_iota(jnp.int32, (ROWS_C, depth), 1) == cols).astype(F32).astype(BF16)
        rows = jnp.dot(picked, pool, preferred_element_type=F32)
        for i in range(PAD):
            store(c, i, rows[i * PAD * SIDE : (i + 1) * PAD * SIDE])


def region_store(out_ref, lead=()):
    def store(c, i, plane):
        for b in range(3):
            out_ref[lead + (b, c, i)] = plane[b * SIDE : b * SIDE + SLAB].astype(BF16)

    return store


def region_kernel(cols_ref, block_ref, slabs_ref, pick_ref, region_ref, *sliced_refs):
    pool = jnp.concatenate([block_ref[...], slabs_ref[...]], axis=0)
    place_region(cols_ref, 0, pool, region_store(region_ref))
    lanes = sliced_refs[0].shape[1]
    for n, ref in enumerate(sliced_refs):
        ref[...] = jnp.dot(
            pool, pick_ref[:, n * lanes : (n + 1) * lanes], preferred_element_type=F32
        ).astype(BF16)


def make_region(cols, block, slabs, pick, count):
    channels = block.shape[1]
    depth = block.shape[0] + slabs.shape[0]
    lanes = pick.shape[1] // count
    return pl.pallas_call(
        region_kernel,
        out_shape=[jax.ShapeDtypeStruct((3, 3, PAD, SLAB, channels), BF16)]
        + [jax.ShapeDtypeStruct((depth, lanes), BF16)] * count,
        in_specs=[vmem()] * 4,
        out_specs=[vmem()] * (count + 1),
        compiler_params=params(),
        cost_estimate=cost(2 * ROWS * depth * channels, 8 * ROWS * channels),
        name="make_region",
    )(cols, block, slabs, pick)


def slices_kernel(count, cols_ref, *refs):
    out_ref = refs[-1]
    for w in range(count):
        place_region(cols_ref, w * ROWS, refs[w][...], region_store(out_ref, (w,)))


def make_slices(cols, pools):
    depth, lanes = pools[0].shape
    count = len(pools)
    return pl.pallas_call(
        functools.partial(slices_kernel, count),
        out_shape=jax.ShapeDtypeStruct((count, 3, 3, PAD, SLAB, lanes), BF16),
        in_specs=[vmem()] * (count + 1),
        out_specs=vmem(),
        compiler_params=params(),
        cost_estimate=cost(2 * count * ROWS * depth * lanes, 8 * count * ROWS * lanes),
        name="make_slices",
    )(cols, *pools)


def weight_copies(spans, me_ref, piece_refs, weight_ref, sems):
    copies = [[] for _ in range(STEPS)]
    for n, (ref, (first, xor)) in enumerate(zip(piece_refs, spans)):
        offs, rows = ref.shape[0], ref.shape[1]
        at = 0 if rows == weight_ref.shape[1] else pl.multiple_of((me_ref[0] ^ xor) * rows, 16)
        for t in range(first // 3, (first + offs) // 3):
            copies[t].append(
                pltpu.make_async_copy(
                    ref.at[pl.ds(3 * t - first, 3)],
                    weight_ref.at[pl.ds(3 * t, 3), pl.ds(at, rows), :],
                    sems.at[n, t],
                )
            )
    return copies


def forward_kernel(spans, me_ref, region_ref, cot_ref, mask_ref, take_ref, *refs):
    pieces = refs[: len(spans)]
    delta_ref, turned_ref, slabs_ref, weight_ref, total_ref, sems = refs[len(spans) :]
    copies = weight_copies(spans, me_ref, pieces, weight_ref, sems)
    for step in copies:
        for copy in step:
            copy.start()
    channels = weight_ref.shape[1]
    for t in range(STEPS):
        for copy in copies[t]:
            copy.wait()
        a, b = t // 3, t % 3
        left = jnp.concatenate(
            [region_ref[b, c, a : a + SIDE].reshape(VOX, channels) for c in range(3)], axis=1
        )
        right = weight_ref[3 * t : 3 * t + 3].reshape(3 * channels, weight_ref.shape[2])
        part = jnp.dot(left, right, preferred_element_type=F32)
        total_ref[...] = part if t == 0 else total_ref[...] + part
    pre = total_ref[...]
    gate = jax.nn.sigmoid(pre)
    delta = cot_ref[...].astype(F32) * mask_ref[...] * gate * (1.0 + pre * (1.0 - gate))
    delta = delta.astype(BF16)
    delta_ref[...] = delta
    turned_ref[...] = delta.astype(F32).T.astype(BF16)
    slabs_ref[...] = jnp.dot(take_ref[...], delta, preferred_element_type=F32).astype(BF16)


def forward(spans, me, region, cot, mask, take, pieces):
    channels = region.shape[-1]
    cout = cot.shape[1]
    return pl.pallas_call(
        functools.partial(forward_kernel, spans),
        out_shape=[
            jax.ShapeDtypeStruct((VOX, cout), BF16),
            jax.ShapeDtypeStruct((cout, VOX), BF16),
            jax.ShapeDtypeStruct((take.shape[0], cout), BF16),
        ],
        in_specs=[pl.BlockSpec(memory_space=pltpu.SMEM)]
        + [vmem()] * 4
        + [pl.BlockSpec(memory_space=pl.ANY)] * len(pieces),
        out_specs=[vmem()] * 3,
        scratch_shapes=[
            pltpu.VMEM((OFFS, channels, cout), BF16),
            pltpu.VMEM((VOX, cout), F32),
            pltpu.SemaphoreType.DMA((len(pieces), STEPS)),
        ],
        compiler_params=params(),
        cost_estimate=cost(2 * VOX * OFFS * channels * cout, 3 * OFFS * channels * cout),
        name="forward",
    )(me, region, cot, mask, take, *pieces)


def backward_kernel(spans, me_ref, cols_ref, delta_ref, slabs_ref, mask_ref, *refs):
    pieces = refs[: len(spans)]
    back_ref, weight_ref, region_ref, total_ref, sems = refs[len(spans) :]
    copies = weight_copies(spans, me_ref, pieces, weight_ref, sems)
    for step in copies:
        for copy in step:
            copy.start()
    pool = jnp.concatenate([delta_ref[...], slabs_ref[...]], axis=0)
    place_region(cols_ref, 0, pool, region_store(region_ref))
    cout = weight_ref.shape[2]
    for t in range(STEPS):
        for copy in copies[t]:
            copy.wait()
        a, b = 2 - t // 3, 2 - t % 3
        left = jnp.concatenate(
            [region_ref[b, 2 - c, a : a + SIDE].reshape(VOX, cout) for c in range(3)], axis=1
        )
        right = jnp.concatenate([weight_ref[3 * t + c] for c in range(3)], axis=1)
        part = lax.dot_general(left, right, (((1,), (1,)), ((), ())), preferred_element_type=F32)
        total_ref[...] = part if t == 0 else total_ref[...] + part
    back_ref[...] = (mask_ref[...] * total_ref[...]).astype(BF16)


def backward(spans, me, cols, delta, slabs, mask, pieces, channels):
    cout = delta.shape[1]
    return pl.pallas_call(
        functools.partial(backward_kernel, spans),
        out_shape=jax.ShapeDtypeStruct((VOX, channels), BF16),
        in_specs=[pl.BlockSpec(memory_space=pltpu.SMEM)]
        + [vmem()] * 4
        + [pl.BlockSpec(memory_space=pl.ANY)] * len(pieces),
        out_specs=vmem(),
        scratch_shapes=[
            pltpu.VMEM((OFFS, channels, cout), BF16),
            pltpu.VMEM((3, 3, PAD, SLAB, cout), BF16),
            pltpu.VMEM((VOX, channels), F32),
            pltpu.SemaphoreType.DMA((len(pieces), STEPS)),
        ],
        compiler_params=params(),
        cost_estimate=cost(2 * VOX * OFFS * channels * cout, 3 * OFFS * channels * cout),
        name="backward",
    )(me, cols, delta, slabs, mask, *pieces)


def pack_lanes(parts, width, half):
    count = len(parts)
    tiles = [None] * (-(-count * width // LANES))
    lane = lax.broadcasted_iota(jnp.int32, parts[0].shape, 1)
    for n, part in enumerate(parts):
        goal = n * width
        shift = (goal - half * width) % LANES
        moved = pltpu.roll(part, shift, 1) if shift else part
        for tile in range(goal // LANES, (goal + width - 1) // LANES + 1):
            low, high = goal - tile * LANES, goal + width - tile * LANES
            kept = jnp.where((lane >= low) & (lane < high), moved, 0.0)
            tiles[tile] = kept if tiles[tile] is None else tiles[tile] + kept
    return tiles


def gradient_kernel(count, width, halves, first, steps, *refs):
    turned = refs[:count]
    slices_ref = refs[count]
    outs = refs[count + 1 :]
    parts = []
    for t0 in range(first, first + steps, 2):
        ts = range(t0, min(t0 + 2, first + steps))
        total = None
        for w in range(count):
            right = jnp.concatenate(
                [
                    slices_ref[w, t % 3, c, t // 3 : t // 3 + SIDE].reshape(VOX, LANES)
                    for t in ts
                    for c in range(3)
                ],
                axis=1,
            )
            part = jnp.dot(turned[w][...], right, preferred_element_type=F32)
            total = part if total is None else total + part
        parts += [total[:, LANES * n : LANES * (n + 1)] for n in range(3 * len(ts))]
    for half in range(halves):
        for tile, value in enumerate(pack_lanes(parts, width, half)):
            outs[half][:, LANES * tile : LANES * (tile + 1)] = value.astype(outs[half].dtype)


def gradient(turned, slices, width, halves, first, steps):
    cout = turned[0].shape[0]
    count = len(turned)
    lanes = -(-3 * steps * width // LANES) * LANES
    return pl.pallas_call(
        functools.partial(gradient_kernel, count, width, halves, first, steps),
        out_shape=[jax.ShapeDtypeStruct((cout, lanes), BF16)] * (halves - 1)
        + [jax.ShapeDtypeStruct((cout, lanes), F32)],
        in_specs=[vmem()] * (count + 1),
        out_specs=[vmem()] * halves,
        compiler_params=params(),
        cost_estimate=cost(2 * count * cout * VOX * 3 * steps * LANES, 8 * cout * lanes),
        name="gradient",
    )(*turned, slices)


def update_kernel(chunks, width, per_chunk, *refs):
    n_in = len(chunks) * per_chunk
    first_ref, second_ref, new_first_ref, new_second_ref, grad_ref = refs[n_in:]
    for n, (first, steps) in enumerate(chunks):
        total = None
        for ref in refs[n * per_chunk : (n + 1) * per_chunk]:
            value = ref[...].astype(F32)
            total = value if total is None else total + value
        short = LANES - total.shape[0]
        if short:
            total = jnp.concatenate([total, jnp.zeros((short, total.shape[1]), F32)], axis=0)
        rows = total.T
        for k in range(3 * steps):
            grad_ref[pl.ds(3 * first + k, width, stride=OFFS), :] = rows[k * width : (k + 1) * width]
    grad = grad_ref[:, : first_ref.shape[1]] / 64.0
    new_first_ref[...] = 0.9 * first_ref[...] + 0.1 * grad
    new_second_ref[...] = 0.999 * second_ref[...] + 0.001 * grad * grad


def update(chunks, width, partials, first_moment, second_moment):
    flat = [p for group in partials for p in group]
    shape = first_moment.shape
    return pl.pallas_call(
        functools.partial(update_kernel, chunks, width, len(partials[0])),
        out_shape=[jax.ShapeDtypeStruct(shape, F32)] * 2,
        in_specs=[vmem()] * (len(flat) + 2),
        out_specs=[vmem()] * 2,
        scratch_shapes=[pltpu.VMEM((shape[0], LANES), F32)],
        compiler_params=params(),
        cost_estimate=cost(0, 20 * shape[0] * shape[1]),
        name="update",
    )(*flat, first_moment, second_moment)


def swap(x, dp, bit):
    return lax.ppermute(x, "dp", [(i, i ^ bit) for i in range(dp)])


def gather_weight(own, dp, pool):
    if dp // pool == 4 and pool == 2:
        cut = 15
        x_bit, y_bit = pool, 2 * pool
        from_x, from_y = swap(own, dp, x_bit), swap(own, dp, y_bit)
        diag_x = swap(from_y[:cut], dp, x_bit)
        diag_y = swap(from_x[cut:], dp, y_bit)
        pieces = [
            (own, 0, 0),
            (from_x, 0, x_bit),
            (from_y, 0, y_bit),
            (diag_x, 0, x_bit | y_bit),
            (diag_y, cut, x_bit | y_bit),
        ]
        return pieces + [(swap(arr, dp, 1), first, xor | 1) for arr, first, xor in pieces]
    pieces = [(own, 0, 0)]
    bit = 1
    while bit < dp:
        pieces += [(swap(arr, dp, bit), first, xor | bit) for arr, first, xor in pieces]
        bit *= 2
    return pieces


def whole_weight(pieces, me, dp):
    stacked = jnp.stack([arr for arr, _, _ in sorted(pieces, key=lambda p: p[2])], axis=0)
    order = jnp.arange(dp) ^ me
    ordered = jnp.take(stacked, order, axis=0)
    joined = ordered.transpose(1, 0, 2, 3).reshape(OFFS, -1, stacked.shape[-1])
    return [(joined, 0, 0)]


def body(features, cotangent, weight, occupancy, neighbours, first_moment, second_moment):
    capacity, channels = features.shape[1], features.shape[3]
    spatial = lax.axis_size("space")
    dp = lax.axis_size("dp")
    group = capacity * spatial
    pool = 2 if dp % 2 == 0 else 1
    teams = dp // pool
    width = channels // dp
    cout_here = first_moment.shape[1]
    if capacity != 2 or features.shape[0] != 1:
        raise ValueError("unsupported sizes")
    me = lax.axis_index("dp")
    z = lax.axis_index("space")
    hops = hop_pairs(spatial, capacity)

    table = neighbours[0]
    slot_ids = jnp.arange(group, dtype=jnp.int32)
    present = table[:, 13] >= 0
    ranking = jnp.cumsum(present.astype(jnp.int32)) - 1
    ranks = jnp.arange(spatial, dtype=jnp.int32)
    is_rank = present[None, :] & (ranking[None, :] == ranks[:, None])
    slot_of = jnp.sum(jnp.where(is_rank, slot_ids[None, :], 0), axis=1)
    rank_rows = jnp.sum(jnp.where(is_rank[:, :, None], table[None], 0), axis=1)
    rank_of = jnp.sum(
        jnp.where(
            (rank_rows[:, :, None] == slot_ids) & present, ranking[None, None, :] + 1, 0
        ),
        axis=2,
    ) - 1
    mine = ranks == z
    my_slot = jnp.sum(jnp.where(mine, slot_of, 0))
    my_ranks = jnp.sum(jnp.where(mine[:, None], rank_of, 0), axis=0)[None]

    def columns(links):
        rank = jnp.sum(
            jnp.where(ROW_CODE[:, None] == np.arange(OFFS)[None, :], links, 0), axis=1, keepdims=True
        )
        turn = lax.rem(z - rank + spatial, spatial)
        halo = VOX + SLAB * (turn - 1) + ROW_PLACE[:, None]
        return jnp.where(
            ROW_CODE[:, None] == 13, ROW_VOXEL[:, None], jnp.where(rank >= 0, halo, -1)
        ).astype(jnp.int32)

    places = np.arange(SLAB, dtype=np.int32)
    taken = []
    for turn in range(1, spatial):
        links = jnp.sum(
            jnp.where((ranks == lax.rem(z + turn, spatial))[:, None], rank_of, 0), axis=0
        )
        hit = links == z
        code = jnp.sum(jnp.where(hit, jnp.arange(OFFS, dtype=jnp.int32), 0))
        rest, voxel = places, 0
        for axis, step in ((code % 3, 1), (code // 3 % 3, SIDE), (code // 9, SIDE * SIDE)):
            free = axis == 1
            at = jnp.where(free, rest % SIDE, jnp.where(axis == 0, SIDE - 1, 0))
            rest = jnp.where(free, rest // SIDE, rest)
            voxel = voxel + step * at
        taken.append(jnp.where(jnp.any(hit) & (rest == 0), voxel, -1))
    take = (jnp.concatenate(taken)[:, None] == jnp.arange(VOX, dtype=jnp.int32)[None, :]).astype(BF16)

    occ_row = jnp.sum(
        jnp.where((slot_ids == my_slot)[:, None], occupancy[0], 0), axis=0
    )
    mask = occ_row.astype(F32)[:, None]

    own_weight = shuffle_weight(weight)
    pieces = gather_weight(own_weight, dp, pool)
    if width % 16:
        pieces = whole_weight(pieces, me, dp)
    spans = tuple((first, xor) for _, first, xor in pieces)
    piece_arrays = [arr for arr, _, _ in pieces]

    def to_handlers(blocks, after=None):
        arrived = {}
        for dist, pairs in hops.items():
            goal = z - dist
            slot = jnp.sum(jnp.where(ranks == goal, slot_of, 0))
            sent = lax.dynamic_index_in_dim(blocks, slot % capacity, 0, keepdims=False)
            if after is not None:
                sent, _ = lax.optimization_barrier((sent, after))
            arrived[dist] = lax.ppermute(sent, "space", pairs)
        here = my_slot // capacity - z
        out = lax.dynamic_index_in_dim(blocks, my_slot % capacity, 0, keepdims=False)
        for dist, block in arrived.items():
            out = jnp.where(here == dist, block, out)
        return out, arrived

    def exchange_slabs(slabs):
        got = [
            lax.ppermute(
                slabs[(turn - 1) * SLAB : turn * SLAB],
                "space",
                [(i, (i + turn) % spatial) for i in range(spatial)],
            )
            for turn in range(1, spatial)
        ]
        return jnp.concatenate(got, axis=0)

    block, x_arrived = to_handlers(features[0])
    block = block * mask.astype(BF16)
    cot, _ = to_handlers(cotangent[0], [x[:1, :1] for x in x_arrived.values()])
    x_slabs = jnp.dot(take, block, preferred_element_type=F32).astype(BF16)
    x_slabs = exchange_slabs(x_slabs)

    cols = columns(my_ranks)
    lanes = -(-pool * width // LANES) * LANES
    lane = jnp.arange(teams * lanes, dtype=jnp.int32)
    team, color = me // pool, me % pool
    inner = lane % lanes
    part = inner // width
    owner_color = part ^ (color ^ (pool - 1))
    channel = ((team ^ (lane // lanes)) * pool + owner_color) * width + inner % width
    channel = jnp.where(inner < pool * width, channel, -1)
    pick = (jnp.arange(channels, dtype=jnp.int32)[:, None] == channel[None, :]).astype(BF16)
    region, *sliced = make_region(cols, block, x_slabs, pick, teams)

    me_scalar = me[None].astype(jnp.int32)
    delta, turned, d_slabs = forward(spans, me_scalar, region, cot, mask, take, piece_arrays)

    all_links = [my_ranks] + [swap(my_ranks, dp, e * pool) for e in range(1, teams)]
    pools = [sliced[0]] + [swap(sliced[e], dp, e * pool) for e in range(1, teams)]
    all_cols = jnp.concatenate([columns(links) for links in all_links], axis=0)
    slices = make_slices(all_cols, pools)
    turned_all = [turned] + [swap(turned, dp, e * pool) for e in range(1, teams)]

    d_slabs = exchange_slabs(d_slabs)
    back = backward(spans, me_scalar, cols, delta, d_slabs, mask, piece_arrays, channels)
    returned = {
        dist: lax.ppermute(back, "space", [(h, o) for o, h in pairs]) for dist, pairs in hops.items()
    }
    own_grads = []
    for n in range(capacity):
        slot = z * capacity + n
        here = slot_ids == slot
        live = jnp.any(here & present)
        dist = z - jnp.sum(jnp.where(here, ranking, 0))
        value = back
        for d, arr in returned.items():
            value = jnp.where(dist == d, arr, value)
        value = jnp.where(live, value.astype(F32), 0.0)
        own_grads.append((cotangent[0, n].astype(F32) + value).astype(BF16))
    input_grad = jnp.stack(own_grads)[None]

    chunks = ((0, 4), (4, 5))
    partials = []
    for first, steps in chunks:
        *sent, kept = gradient(turned_all, slices, width, pool, first, steps)
        for arr in sent:
            kept = kept + swap(arr, dp, 1).astype(F32)
        summed = kept.astype(BF16)
        mine_rows = lax.dynamic_slice_in_dim(kept, z * cout_here, cout_here, 0)
        group_parts = [mine_rows]
        for turn in range(1, spatial):
            goal = lax.rem(z + turn, spatial)
            rows = lax.dynamic_slice_in_dim(summed, goal * cout_here, cout_here, 0)
            group_parts.append(
                lax.ppermute(rows, "space", [(i, (i + turn) % spatial) for i in range(spatial)])
            )
        partials.append(group_parts)
    new_first, new_second = update(chunks, width, partials, first_moment, second_moment)
    return input_grad, new_first, new_second


def solution(mesh):
    return jax.shard_map(
        body,
        mesh=mesh,
        in_specs=(
            P("dp", "space", None, None),
            P("dp", "space", None, None),
            P("dp", None),
            P("dp", None, None),
            P("dp", None, None),
            P("dp", "space"),
            P("dp", "space"),
        ),
        out_specs=(P("dp", "space", None, None), P("dp", "space"), P("dp", "space")),
        check_vma=False,
    )
```

```python
import functools
import itertools

import jax
import jax.numpy as jnp
import numpy as np
from jax import lax
from jax.experimental import pallas as pl
from jax.experimental.pallas import tpu as pltpu
from jax.sharding import PartitionSpec as P


SIDE = 8
PAD = SIDE + 2
VOX = SIDE**3
OFFS = 27
SLAB = SIDE * SIDE
STEPS = 9
CUT = 15
GROUPS = ((0, 2), (2, 5), (5, STEPS))
CHUNKS = ((0, 3), (3, 6))
LANES = 128
F32 = jnp.float32
BF16 = jnp.bfloat16


def hop_pairs(spatial, capacity):
    group = spatial * capacity
    live = group // 2
    pairs = {}
    for chosen in itertools.combinations(range(group - 1), live - 1):
        slots = chosen + (group - 1,)
        counts = np.bincount([s // capacity for s in slots], minlength=spatial)
        if counts.max() < capacity:
            continue
        for rank, slot in enumerate(slots):
            owner = slot // capacity
            if owner != rank:
                pairs.setdefault(owner - rank, set()).add((owner, rank))
    return {dist: sorted(found) for dist, found in sorted(pairs.items())}


def region_rows():
    c, i, j, l = np.meshgrid(range(3), range(PAD), range(PAD), range(SIDE), indexing="ij")
    coords = (i, j, l + c)
    edges = [np.where(x == 0, 0, np.where(x == PAD - 1, 2, 1)) for x in coords]
    source = [(x - 1) % SIDE for x in coords]
    code = 9 * edges[0] + 3 * edges[1] + edges[2]
    place = np.zeros_like(code)
    for x, e in zip(source, edges):
        place = np.where(e == 1, place * SIDE + x, place)
    return tuple(t.reshape(3, -1).astype(np.int32) for t in (code, place))


ROW_CODE, ROW_PLACE = region_rows()
ROWS_C = ROW_CODE.shape[1]
NOWHERE = -4096


def vmem():
    return pl.BlockSpec(memory_space=pltpu.VMEM)


def smem():
    return pl.BlockSpec(memory_space=pltpu.SMEM)


def hbm():
    return pl.BlockSpec(memory_space=pl.ANY)


def params(mib=48):
    return pltpu.CompilerParams(vmem_limit_bytes=mib * 1024 * 1024)


def cost(flops, nbytes):
    return pl.CostEstimate(flops=int(flops), bytes_accessed=int(nbytes), transcendentals=0)


def live_ranks(table_ref):
    seen, live, rank = jnp.int32(0), [], []
    for s in range(table_ref.shape[0]):
        here = table_ref[s, 13] >= 0
        live.append(here)
        rank.append(seen)
        seen = seen + here.astype(jnp.int32)
    return live, rank


def slot_of(goal, live, rank):
    found = jnp.int32(0)
    for s, (here, r) in enumerate(zip(live, rank)):
        found = jnp.where(here & (r == goal), s, found)
    return found


def from_owner(capacity, table_ref, own_ref, dists, arrived, dest, sem):
    z = lax.axis_index("space")
    slot = slot_of(z, *live_ranks(table_ref))
    away = slot // capacity - z
    choices = [(away == 0, pltpu.make_async_copy(own_ref.at[slot % capacity], dest, sem))]
    for dist, ref in zip(dists, arrived):
        choices.append((away == dist, pltpu.make_async_copy(ref, dest, sem)))
    return choices


def start_all(choices):
    for cond, copy in choices:
        pl.when(cond)(copy.start)


def wait_all(choices):
    for cond, copy in choices:
        pl.when(cond)(copy.wait)


def shuffle_kernel(cuts, w_ref, *refs):
    outs, wide = refs[:-1], refs[-1]
    rows = outs[0].shape[1]
    for tile in range(wide.shape[0]):
        lanes = slice(tile * LANES, (tile + 1) * LANES)
        wide[tile] = w_ref[:, lanes].astype(F32)
        for out, (first, last) in zip(outs, cuts):
            for k in range(first, last):
                out[k - first, :, lanes] = wide[tile, pl.ds(k, rows, stride=OFFS), :].astype(BF16)


def shuffle_weight(weight, cuts):
    rows, cout = weight.shape
    return pl.pallas_call(
        functools.partial(shuffle_kernel, cuts),
        out_shape=[jax.ShapeDtypeStruct((last - first, rows // OFFS, cout), BF16) for first, last in cuts],
        in_specs=[vmem()],
        out_specs=[vmem()] * len(cuts),
        scratch_shapes=[pltpu.VMEM((cout // LANES, rows, LANES), F32)],
        compiler_params=params(16),
        cost_estimate=cost(0, 4 * rows * cout),
        name="shuffle_weight",
    )(weight)


def outgoing_kernel(dists, table_ref, blocks_ref, *outs):
    z = lax.axis_index("space")
    capacity = blocks_ref.shape[0]
    live, rank = live_ranks(table_ref)
    for dist, out in zip(dists, outs):
        slot = slot_of(z - dist, live, rank)
        out[...] = blocks_ref[slot % capacity]


def outgoing(dists, table, blocks):
    return pl.pallas_call(
        functools.partial(outgoing_kernel, dists),
        out_shape=[jax.ShapeDtypeStruct(blocks.shape[1:], blocks.dtype)] * len(dists),
        in_specs=[smem(), vmem()],
        out_specs=[vmem()] * len(dists),
        compiler_params=params(16),
        cost_estimate=cost(0, 10 * blocks.size),
        name="outgoing",
    )(table, blocks)


def receive_kernel(dists, spatial, capacity, table_ref, own_ref, occ_ref, code_ref, place_ref, *refs):
    arrived = refs[: len(dists)]
    block_ref, mask_ref, take_ref, cols_ref, *slab_refs = refs[len(dists) : -3]
    raw, rank_ref, sem = refs[-3:]
    choices = from_owner(capacity, table_ref, own_ref, dists, arrived, raw, sem)
    start_all(choices)
    z = lax.axis_index("space")
    live, rank = live_ranks(table_ref)
    for s, r in enumerate(rank):
        rank_ref[s] = r
    slot = slot_of(z, live, rank)

    cols = jnp.full(code_ref.shape, NOWHERE, jnp.int32)
    for k in range(OFFS):
        if k == 13:
            continue
        near = table_ref[slot, k]
        turn = lax.rem(z - rank_ref[jnp.maximum(near, 0)] + spatial, spatial)
        base = jnp.where(near >= 0, SLAB * (turn - 1), NOWHERE)
        cols = jnp.where(code_ref[...] == k, base + place_ref[...], cols)
    cols_ref[...] = cols

    voxel = lax.broadcasted_iota(jnp.int32, (1, VOX), 1)
    spots = (voxel // (SIDE * SIDE), voxel // SIDE % SIDE, voxel % SIDE)
    rows = lax.broadcasted_iota(jnp.int32, (SLAB, VOX), 0)
    for turn in range(1, spatial):
        other = slot_of(lax.rem(z + turn, spatial), live, rank)
        code = jnp.int32(-1)
        for k in range(OFFS):
            if k != 13:
                code = jnp.where(table_ref[other, k] == slot, k, code)
        inside = jnp.broadcast_to(code >= 0, (1, VOX))
        place = jnp.zeros((1, VOX), jnp.int32)
        for at, edge in zip(spots, (code // 9, code // 3 % 3, code % 3)):
            fixed = jnp.where(edge == 0, SIDE - 1, 0)
            free = edge == 1
            inside = inside & (free | (at == fixed))
            place = jnp.where(free, place * SIDE + at, place)
        place = jnp.where(inside, place, -1)
        take_ref[(turn - 1) * SLAB : turn * SLAB, :] = (rows == place).astype(F32).astype(BF16)

    occ = occ_ref[pl.ds(slot, 1), :].astype(F32)
    mask = jnp.broadcast_to(occ, (LANES, VOX)).T
    mask_ref[...] = mask
    wait_all(choices)
    channels = raw.shape[1]
    block = (raw[...].astype(F32) * wide_mask(mask, channels)).astype(BF16)
    block_ref[...] = block
    give_slabs(take_ref[...], block, slab_refs)


def wide_mask(mask, channels):
    return jnp.concatenate([mask] * (channels // LANES), axis=1)


def give_slabs(take, block, slab_refs):
    slabs = jnp.dot(take, block, preferred_element_type=F32).astype(BF16)
    for n, ref in enumerate(slab_refs):
        ref[...] = slabs[n * SLAB : (n + 1) * SLAB]


def receive(dists, spatial, table, own, occupancy, arrived):
    channels = own.shape[2]
    turns = spatial - 1
    return pl.pallas_call(
        functools.partial(receive_kernel, dists, spatial, own.shape[0]),
        out_shape=[
            jax.ShapeDtypeStruct((VOX, channels), BF16),
            jax.ShapeDtypeStruct((VOX, LANES), F32),
            jax.ShapeDtypeStruct((turns * SLAB, VOX), BF16),
            jax.ShapeDtypeStruct(ROW_CODE.shape, jnp.int32),
        ]
        + [jax.ShapeDtypeStruct((SLAB, channels), BF16)] * turns,
        in_specs=[smem(), hbm(), vmem(), vmem(), vmem()] + [hbm()] * len(arrived),
        out_specs=[vmem()] * (4 + turns),
        scratch_shapes=[
            pltpu.VMEM((VOX, channels), BF16),
            pltpu.SMEM((table.shape[0],), jnp.int32),
            pltpu.SemaphoreType.DMA,
        ],
        compiler_params=params(16),
        cost_estimate=cost(2 * turns * SLAB * VOX * channels, 8 * VOX * channels),
        name="receive",
    )(table, own, occupancy, ROW_CODE, ROW_PLACE, *arrived)


def place_region(cols, block, slabs, out_ref, lead=()):
    depth, channels = slabs.shape
    block = block.astype(F32)
    level = lax.broadcasted_iota(jnp.int32, (VOX, channels), 0) % SIDE
    for c in range(3):
        picked = lax.broadcasted_iota(jnp.int32, (depth, ROWS_C), 0) == cols[c : c + 1, :]
        halo = lax.dot_general(
            picked.astype(F32).astype(BF16), slabs, (((0,), (0,)), ((), ())), preferred_element_type=F32
        )
        inner = block
        if c == 0:
            inner = jnp.where(level == 0, 0.0, pltpu.roll(block, 1, 0))
        if c == 2:
            inner = jnp.where(level == SIDE - 1, 0.0, pltpu.roll(block, VOX - 1, 0))
        for i in range(PAD):
            plane = halo[i * PAD * SIDE : (i + 1) * PAD * SIDE]
            if 0 < i < PAD - 1:
                middle = plane[SIDE : SIDE + SLAB] + inner[(i - 1) * SLAB : i * SLAB]
                plane = jnp.concatenate([plane[:SIDE], middle, plane[SIDE + SLAB :]], axis=0)
            for b in range(3):
                out_ref[lead + (b, c, i)] = plane[b * SIDE : b * SIDE + SLAB].astype(BF16)


def make_region_kernel(turns, width, pool, cols_ref, block_ref, *refs):
    slab_refs, region_ref, sliced_refs = refs[:turns], refs[turns], refs[turns + 1 :]
    slabs = jnp.concatenate([ref[...] for ref in slab_refs], axis=0)
    channels = block_ref.shape[1]
    lanes = sliced_refs[0].shape[1]
    me = lax.axis_index("dp")
    team, color = me // pool, me % pool
    lane = lax.broadcasted_iota(jnp.int32, (channels, lanes), 1)
    row = lax.broadcasted_iota(jnp.int32, (channels, lanes), 0)
    part = lane // width
    inner = (part ^ (color ^ (pool - 1))) * width + lane % width
    for e, ref in enumerate(sliced_refs):
        start = (team ^ e) * (pool * width)
        pick = (part < pool) & (row == start + inner)
        pick = pick.astype(F32).astype(BF16)
        ref[:VOX] = jnp.dot(block_ref[...], pick, preferred_element_type=F32).astype(BF16)
        ref[VOX:] = jnp.dot(slabs, pick, preferred_element_type=F32).astype(BF16)
    place_region(cols_ref[...], block_ref[...], slabs, region_ref)


def make_region(cols, block, slabs, teams, width, pool):
    channels = block.shape[1]
    depth = VOX + len(slabs) * SLAB
    lanes = -(-pool * width // LANES) * LANES
    return pl.pallas_call(
        functools.partial(make_region_kernel, len(slabs), width, pool),
        out_shape=[jax.ShapeDtypeStruct((3, 3, PAD, SLAB, channels), BF16)]
        + [jax.ShapeDtypeStruct((depth, lanes), BF16)] * teams,
        in_specs=[vmem()] * (2 + len(slabs)),
        out_specs=[vmem()] * (teams + 1),
        compiler_params=params(32),
        cost_estimate=cost(2 * 3 * ROWS_C * 192 * channels, 24 * ROWS_C * channels),
        name="make_region",
    )(cols, block, *slabs)


def slices_kernel(count, *refs):
    out_ref = refs[-1]
    for w in range(count):
        both = refs[count + w]
        place_region(refs[w][...], both[:VOX], both[VOX:], out_ref, (w,))


def make_slices(cols, pools):
    lanes = pools[0].shape[1]
    count = len(pools)
    return pl.pallas_call(
        functools.partial(slices_kernel, count),
        out_shape=jax.ShapeDtypeStruct((count, 3, 3, PAD, SLAB, lanes), BF16),
        in_specs=[vmem()] * (2 * count),
        out_specs=vmem(),
        compiler_params=params(32),
        cost_estimate=cost(2 * count * 3 * ROWS_C * 192 * lanes, 24 * count * ROWS_C * lanes),
        name="make_slices",
    )(*cols, *pools)


def weight_copies(spans, piece_refs, weight_ref, sems):
    copies = []
    me = lax.axis_index("dp")
    for g, (low, high) in enumerate(GROUPS):
        group = []
        for n, (ref, (first, xor)) in enumerate(zip(piece_refs, spans)):
            offs, rows = ref.shape[0], ref.shape[1]
            at = 0 if rows == weight_ref.shape[1] else pl.multiple_of((me ^ xor) * rows, 16)
            start, stop = max(3 * low, first), min(3 * high, first + offs)
            if start < stop:
                group.append(
                    pltpu.make_async_copy(
                        ref.at[pl.ds(start - first, stop - start)],
                        weight_ref.at[pl.ds(start, stop - start), pl.ds(at, rows), :],
                        sems.at[n, g],
                    )
                )
        copies.append(group)
    return copies


def forward_kernel(spans, dists, capacity, table_ref, region_ref, mask_ref, take_ref, own_ref, *refs):
    arrived, refs = refs[: len(dists)], refs[len(dists) :]
    pieces, refs = refs[: len(spans)], refs[len(spans) :]
    delta_ref, *slab_refs, weight_ref, total_ref, cot_ref, cot_sem, sems = refs
    copies = weight_copies(spans, pieces, weight_ref, sems)
    for group in copies:
        for copy in group:
            copy.start()
    choices = from_owner(capacity, table_ref, own_ref, dists, arrived, cot_ref, cot_sem)
    start_all(choices)
    channels = weight_ref.shape[1]
    total_ref[...] = jnp.zeros_like(total_ref)

    def step(t, _):
        a, b = t // 3, t % 3
        left = jnp.concatenate(
            [region_ref[b, c, pl.ds(a, SIDE)].reshape(VOX, channels) for c in range(3)], axis=1
        )
        right = weight_ref[pl.ds(3 * t, 3)].reshape(3 * channels, weight_ref.shape[2])
        total_ref[...] += jnp.dot(left, right, preferred_element_type=F32)
        return 0

    for group, (low, high) in zip(copies, GROUPS):
        for copy in group:
            copy.wait()
        lax.fori_loop(low, high, step, 0)
    wait_all(choices)
    pre = total_ref[...]
    gate = jax.nn.sigmoid(pre)
    mask = wide_mask(mask_ref[...], pre.shape[1])
    delta = cot_ref[...].astype(F32) * mask * gate * (1.0 + pre * (1.0 - gate))
    delta = delta.astype(BF16)
    delta_ref[...] = delta
    give_slabs(take_ref[...], delta, slab_refs)


def forward(spans, dists, table, region, mask, take, own, arrived, pieces):
    channels = region.shape[-1]
    capacity, _, cout = own.shape
    turns = take.shape[0] // SLAB
    return pl.pallas_call(
        functools.partial(forward_kernel, spans, dists, capacity),
        out_shape=[jax.ShapeDtypeStruct((VOX, cout), BF16)]
        + [jax.ShapeDtypeStruct((SLAB, cout), BF16)] * turns,
        in_specs=[smem()] + [vmem()] * 3 + [hbm()] * (1 + len(arrived) + len(pieces)),
        out_specs=[vmem()] * (1 + turns),
        scratch_shapes=[
            pltpu.VMEM((OFFS, channels, cout), BF16),
            pltpu.VMEM((VOX, cout), F32),
            pltpu.VMEM((VOX, cout), BF16),
            pltpu.SemaphoreType.DMA,
            pltpu.SemaphoreType.DMA((len(pieces), len(GROUPS))),
        ],
        compiler_params=params(32),
        cost_estimate=cost(2 * VOX * OFFS * channels * cout, 3 * OFFS * channels * cout),
        name="forward",
    )(table, region, mask, take, own, *arrived, *pieces)


def backward_kernel(spans, turns, cols_ref, delta_ref, mask_ref, *refs):
    slab_refs, refs = refs[:turns], refs[turns:]
    pieces, refs = refs[: len(spans)], refs[len(spans) :]
    back_ref, weight_ref, region_ref, total_ref, sems = refs
    copies = weight_copies(spans, pieces, weight_ref, sems)
    for group in copies:
        for copy in group:
            copy.start()
    slabs = jnp.concatenate([ref[...] for ref in slab_refs], axis=0)
    place_region(cols_ref[...], delta_ref[...], slabs, region_ref)
    cout = weight_ref.shape[2]
    total_ref[...] = jnp.zeros_like(total_ref)

    def step(t, _):
        a, b = 2 - t // 3, 2 - t % 3
        left = jnp.concatenate(
            [region_ref[b, 2 - c, pl.ds(a, SIDE)].reshape(VOX, cout) for c in range(3)], axis=1
        )
        right = jnp.concatenate([weight_ref[3 * t + c] for c in range(3)], axis=1)
        total_ref[...] += lax.dot_general(
            left, right, (((1,), (1,)), ((), ())), preferred_element_type=F32
        )
        return 0

    for group, (low, high) in zip(copies, GROUPS):
        for copy in group:
            copy.wait()
        lax.fori_loop(low, high, step, 0)
    back_ref[...] = (wide_mask(mask_ref[...], total_ref.shape[1]) * total_ref[...]).astype(BF16)


def backward(spans, cols, delta, mask, slabs, pieces, channels):
    cout = delta.shape[1]
    return pl.pallas_call(
        functools.partial(backward_kernel, spans, len(slabs)),
        out_shape=jax.ShapeDtypeStruct((VOX, channels), BF16),
        in_specs=[vmem()] * (3 + len(slabs)) + [hbm()] * len(pieces),
        out_specs=vmem(),
        scratch_shapes=[
            pltpu.VMEM((OFFS, channels, cout), BF16),
            pltpu.VMEM((3, 3, PAD, SLAB, cout), BF16),
            pltpu.VMEM((VOX, channels), F32),
            pltpu.SemaphoreType.DMA((len(pieces), len(GROUPS))),
        ],
        compiler_params=params(32),
        cost_estimate=cost(2 * VOX * OFFS * channels * cout, 3 * OFFS * channels * cout),
        name="backward",
    )(cols, delta, mask, *slabs, *pieces)


def pack_lanes(parts, width, half):
    count = len(parts)
    tiles = [None] * (-(-count * width // LANES))
    lane = lax.broadcasted_iota(jnp.int32, parts[0].shape, 1)
    for n, part in enumerate(parts):
        goal = n * width
        shift = (goal - half * width) % LANES
        moved = pltpu.roll(part, shift, 1) if shift else part
        for tile in range(goal // LANES, (goal + width - 1) // LANES + 1):
            low, high = goal - tile * LANES, goal + width - tile * LANES
            kept = jnp.where((lane >= low) & (lane < high), moved, 0.0)
            tiles[tile] = kept if tiles[tile] is None else tiles[tile] + kept
    return tiles


def gradient_kernel(count, width, halves, first, steps, *refs):
    deltas = refs[:count]
    slices_ref = refs[count]
    outs, total_ref = refs[count + 1 : -1], refs[-1]

    def row(a, _):
        total = None
        for w in range(count):
            right = jnp.concatenate(
                [
                    slices_ref[w, b, c, pl.ds(first // 3 + a, SIDE)].reshape(VOX, LANES)
                    for b in range(3)
                    for c in range(3)
                ],
                axis=1,
            )
            part = lax.dot_general(
                deltas[w][...], right, (((0,), (0,)), ((), ())), preferred_element_type=F32
            )
            total = part if total is None else total + part
        total_ref[a] = total
        return 0

    lax.fori_loop(0, steps // 3, row, 0)
    parts = [
        total_ref[a, :, LANES * n : LANES * (n + 1)] for a in range(steps // 3) for n in range(9)
    ]
    for half in range(halves):
        for tile, value in enumerate(pack_lanes(parts, width, half)):
            outs[half][:, LANES * tile : LANES * (tile + 1)] = value.astype(outs[half].dtype)


def gradient(deltas, slices, width, halves, first, steps):
    cout = deltas[0].shape[1]
    count = len(deltas)
    lanes = -(-3 * steps * width // LANES) * LANES
    return pl.pallas_call(
        functools.partial(gradient_kernel, count, width, halves, first, steps),
        out_shape=[jax.ShapeDtypeStruct((cout, lanes), BF16)] * (halves - 1)
        + [jax.ShapeDtypeStruct((cout, lanes), F32)],
        in_specs=[vmem()] * (count + 1),
        out_specs=[vmem()] * halves,
        scratch_shapes=[pltpu.VMEM((steps // 3, cout, 9 * LANES), F32)],
        compiler_params=params(40),
        cost_estimate=cost(2 * count * cout * VOX * 3 * steps * LANES, 8 * cout * lanes),
        name="gradient",
    )(*deltas, slices)


def combine_kernel(spatial, count, *refs):
    kept_ref, others, outs = refs[0], refs[1:count], refs[count:]
    z = lax.axis_index("space")
    rows = outs[0].shape[0]
    for turn, out in enumerate(outs):
        at = pl.ds(pl.multiple_of(lax.rem(z + turn, spatial) * rows, 16), rows)
        value = kept_ref[at, :]
        for ref in others:
            value = value + ref[at, :].astype(F32)
        out[...] = value.astype(out.dtype)


def combine(kept, others, spatial):
    rows, lanes = kept.shape[0] // spatial, kept.shape[1]
    return pl.pallas_call(
        functools.partial(combine_kernel, spatial, 1 + len(others)),
        out_shape=[jax.ShapeDtypeStruct((rows, lanes), F32)]
        + [jax.ShapeDtypeStruct((rows, lanes), BF16)] * (spatial - 1),
        in_specs=[vmem()] * (1 + len(others)),
        out_specs=[vmem()] * spatial,
        compiler_params=params(16),
        cost_estimate=cost(0, 10 * kept.size),
        name="combine",
    )(kept, *others)


def update_kernel(chunks, width, per_chunk, *refs):
    n_in = len(chunks) * per_chunk
    first_ref, second_ref, new_first_ref, new_second_ref, grad_ref = refs[n_in:]
    for n, (first, steps) in enumerate(chunks):
        total = None
        for ref in refs[n * per_chunk : (n + 1) * per_chunk]:
            value = ref[...].astype(F32)
            total = value if total is None else total + value
        short = LANES - total.shape[0]
        if short:
            total = jnp.concatenate([total, jnp.zeros((short, total.shape[1]), F32)], axis=0)
        rows = total.T
        for k in range(3 * steps):
            grad_ref[pl.ds(3 * first + k, width, stride=OFFS), :] = rows[k * width : (k + 1) * width]
    grad = grad_ref[...].T[: first_ref.shape[0]] / 64.0
    new_first_ref[...] = 0.9 * first_ref[...] + 0.1 * grad
    new_second_ref[...] = 0.999 * second_ref[...] + 0.001 * grad * grad


def update(chunks, width, partials, first_moment, second_moment):
    flat = [p for group in partials for p in group]
    shape = first_moment.shape
    return pl.pallas_call(
        functools.partial(update_kernel, chunks, width, len(partials[0])),
        out_shape=[jax.ShapeDtypeStruct(shape, F32)] * 2,
        in_specs=[vmem()] * (len(flat) + 2),
        out_specs=[vmem()] * 2,
        scratch_shapes=[pltpu.VMEM((shape[1], LANES), F32)],
        compiler_params=params(24),
        cost_estimate=cost(0, 20 * shape[0] * shape[1]),
        name="update",
    )(*flat, first_moment, second_moment)


def finish_kernel(dists, table_ref, cot_ref, back_ref, *refs):
    returned, out_ref = refs[:-1], refs[-1]
    capacity = cot_ref.shape[0]
    z = lax.axis_index("space")
    live, rank = live_ranks(table_ref)
    for n in range(capacity):
        away = jnp.int32(NOWHERE)
        for s in range(n, table_ref.shape[0], capacity):
            away = jnp.where((s // capacity == z) & live[s], z - rank[s], away)

        def give(ref, n=n):
            value = cot_ref[n].astype(F32) + ref[...].astype(F32)
            out_ref[n] = value.astype(BF16)

        known = away == NOWHERE
        for dist, ref in zip((0,) + tuple(dists), (back_ref,) + tuple(returned)):
            pl.when(away == dist)(functools.partial(give, ref))

        @pl.when(known)
        def _(n=n):
            out_ref[n] = cot_ref[n]


def finish(dists, table, cotangent, back, returned):
    return pl.pallas_call(
        functools.partial(finish_kernel, dists),
        out_shape=jax.ShapeDtypeStruct(cotangent.shape, BF16),
        in_specs=[smem()] + [vmem()] * (2 + len(returned)),
        out_specs=vmem(),
        compiler_params=params(16),
        cost_estimate=cost(0, 12 * cotangent.size),
        name="finish",
    )(table, cotangent, back, *returned)


def swap(x, dp, bit):
    return lax.ppermute(x, "dp", [(i, i ^ bit) for i in range(dp)])


def gather_weight(own, cuts, dp, pool):
    if len(own) == 2:
        x_bit, y_bit = pool, 2 * pool
        from_x = [swap(arr, dp, x_bit) for arr in own]
        from_y = [swap(arr, dp, y_bit) for arr in own]
        diag = [swap(from_y[0], dp, x_bit), swap(from_x[1], dp, y_bit)]
        sets = ((own, 0), (from_x, x_bit), (from_y, y_bit), (diag, x_bit | y_bit))
        pieces = [(arr, first, xor) for arrs, xor in sets for arr, (first, _) in zip(arrs, cuts)]
        return pieces + [(swap(arr, dp, 1), first, xor | 1) for arr, first, xor in pieces]
    pieces = [(own[0], 0, 0)]
    bit = 1
    while bit < dp:
        pieces += [(swap(arr, dp, bit), first, xor | bit) for arr, first, xor in pieces]
        bit *= 2
    return pieces


def whole_weight(pieces, me, dp):
    stacked = jnp.stack([arr for arr, _, _ in sorted(pieces, key=lambda p: p[2])], axis=0)
    order = jnp.arange(dp) ^ me
    ordered = jnp.take(stacked, order, axis=0)
    joined = ordered.transpose(1, 0, 2, 3).reshape(OFFS, -1, stacked.shape[-1])
    return [(joined, 0, 0)]


def after(value, *others):
    return lax.optimization_barrier((value,) + others)[0]


def body(features, cotangent, weight, occupancy, neighbours, first_moment, second_moment):
    capacity, channels = features.shape[1], features.shape[3]
    spatial = lax.axis_size("space")
    dp = lax.axis_size("dp")
    pool = 2 if dp % 2 == 0 else 1
    teams = dp // pool
    width = channels // dp
    if capacity != 2 or features.shape[0] != 1:
        raise ValueError("unsupported sizes")
    hops = hop_pairs(spatial, capacity)
    dists = tuple(hops)
    table = neighbours[0]

    def rotate(arrays):
        return [
            lax.ppermute(arr, "space", [(i, (i + turn) % spatial) for i in range(spatial)])
            for turn, arr in enumerate(arrays, 1)
        ]

    def to_handlers(sent):
        return [lax.ppermute(arr, "space", hops[dist]) for dist, arr in zip(dists, sent)]

    special = teams == 4 and pool == 2 and width % 16 == 0
    cuts = ((0, CUT), (CUT, OFFS)) if special else ((0, OFFS),)
    own_weight = shuffle_weight(weight, cuts)
    pieces = gather_weight(own_weight, cuts, dp, pool)
    if width % 16:
        pieces = whole_weight(pieces, lax.axis_index("dp"), dp)
    spans = tuple((first, xor) for _, first, xor in pieces)
    piece_arrays = [arr for arr, _, _ in pieces]

    table_next = after(table, own_weight[0])
    x_arrived = to_handlers(outgoing(dists, table_next, features[0]))
    cot_sent = outgoing(dists, table_next, cotangent[0])
    block, mask, take, cols, *x_slabs = receive(
        dists, spatial, table, features[0], occupancy[0], x_arrived
    )
    cot_arrived = to_handlers([after(arr, x_arrived[-1]) for arr in cot_sent])
    x_slabs = rotate(x_slabs)

    region, *sliced = make_region(cols, block, x_slabs, teams, width, pool)
    delta, *d_slabs = forward(
        spans, dists, table, region, mask, take, cotangent[0], cot_arrived, piece_arrays
    )

    all_cols = [cols] + [swap(cols, dp, e * pool) for e in range(1, teams)]
    pools = [sliced[0]] + [swap(sliced[e], dp, e * pool) for e in range(1, teams)]
    slices = make_slices(all_cols, pools)
    deltas = [delta] + [swap(delta, dp, e * pool) for e in range(1, teams)]

    back = backward(spans, cols, delta, mask, rotate(d_slabs), piece_arrays, channels)
    returned = [lax.ppermute(back, "space", [(h, o) for o, h in hops[dist]]) for dist in dists]
    input_grad = finish(dists, table, cotangent[0], back, returned)[None]

    partials = []
    for first, steps in CHUNKS:
        *sent, kept = gradient(deltas, slices, width, pool, first, steps)
        own, *others = combine(kept, [swap(arr, dp, 1) for arr in sent], spatial)
        partials.append([own] + rotate(others))
    new_first, new_second = update(CHUNKS, width, partials, first_moment.T, second_moment.T)
    return input_grad, new_first.T, new_second.T


def solution(mesh):
    return jax.shard_map(
        body,
        mesh=mesh,
        in_specs=(
            P("dp", "space", None, None),
            P("dp", "space", None, None),
            P("dp", None),
            P("dp", None, None),
            P("dp", None, None),
            P("dp", "space"),
            P("dp", "space"),
        ),
        out_specs=(P("dp", "space", None, None), P("dp", "space"), P("dp", "space")),
        check_vma=False,
    )
```
